32 devices in a mesh: wide: 8 (over y, x, core), narrow: 4 (over z).
Axes of the slice: x: 2, y: 2, z: 4, core: 2. Of those that a mesh axis runs over, the one named last changes fastest.
Arguments:
- trajectory: bfloat16 [5, 72, 256, 1024], P(None, None, 'narrow', 'wide'), may hold values from -6 to 6
- innovation: float32 [5, 72, 64, 256], P(None, None, 'narrow', 'wide'), may hold values from -6 to 6
- background: float32 [5, 72, 64, 256], P(None, None, 'narrow', 'wide'), may hold values from -6 to 6
- obs_weight: float32 [72, 64, 256], P(None, 'narrow', 'wide'), may hold values from 0.3 to 3
Outputs:
- analysis: bfloat16 [5, 72, 256, 1024], P(None, None, 'narrow', 'wide')
The draws below stay inside these ranges and needn't reach their ends.
All inputs are finite; a program needn't handle non-finite values.
Results may differ from the reference program's by a relative error of at most 0.001.
Values sent between devices are 32-bit elements; how exact they have to be, the bound alone decides.
A program may use at most 128 MiB of HBM per device.

```python
import math
import jax
import jax.numpy as jnp
from jax import lax

FIELDS = 5
LEVELS = 72
COARSEN = 4
STEPS = 2
ITERS = 1
NLAT = 256
NLON = 1024
NLAT_C = 64
NLON_C = 256


def levels(stream_key, dims, pieces, least, largest):
    factor_of = 1.0
    for axis_at, blocks in pieces:
        draws = jax.random.uniform(jax.random.fold_in(jax.random.fold_in(stream_key, 6), axis_at), (blocks,), jnp.float32, least / len(pieces), largest / len(pieces))
        factor_of = factor_of * jnp.repeat(jnp.exp(draws), dims[axis_at] // blocks).reshape((-1,) + (1,) * (len(dims) - 1 - axis_at))
    return factor_of


def normal_values(rng, extent, deviation, most, split=(), kind=jnp.bfloat16):
    level = levels(rng, extent, split, -0.22, 0.18) if split else 1.0
    drawn = jax.random.normal(rng, extent, jnp.float32) * deviation * level
    return jnp.minimum(jnp.maximum(drawn, -most), most).astype(kind)


def setup_inputs(seed: int = 0) -> dict:
    arg_keys = jax.random.split(jax.random.key(seed), 5)
    return {
        "trajectory": normal_values(arg_keys[0], (FIELDS, LEVELS, NLAT, NLON), 1.0, 6.0, ((2, 4), (3, 8))),
        "innovation": normal_values(arg_keys[1], (FIELDS, LEVELS, NLAT_C, NLON_C), 1.0, 6.0, ((2, 4), (3, 8)), jnp.float32),
        "background": normal_values(arg_keys[2], (FIELDS, LEVELS, NLAT_C, NLON_C), 0.7, 6.0, ((2, 4), (3, 8)), jnp.float32),
        "obs_weight": jnp.clip(jnp.exp(math.log(3.0) - 2.3025851 * jax.random.uniform(arg_keys[3], (LEVELS, NLAT_C, NLON_C), jnp.float32) ** levels(arg_keys[3], (LEVELS, NLAT_C, NLON_C), ((1, 4), (2, 8)), -0.2, 0.2)), 0.3, 3.0),
    }


diffusion = 0.2
advection_scale = 0.3
descent_step = 1.0


def filter_rows(row_index, total_rows, cycle_size):
    wavenumber = jnp.arange(cycle_size, dtype=jnp.int32)
    folded = jnp.minimum(wavenumber, cycle_size - wavenumber).astype(jnp.float32)
    latitude = jnp.pi * ((row_index.astype(jnp.float32) + 0.5) / total_rows - 0.5)
    cutoff = 0.5 * cycle_size * jnp.cos(latitude)
    scaled_wave = folded[None, :] / cutoff[:, None]
    response = 1.0 / (1.0 + scaled_wave ** 4)
    phase_index = (wavenumber[:, None] * wavenumber[None, :]) % cycle_size
    angles = (2.0 * jnp.pi / cycle_size) * phase_index.astype(jnp.float32)
    basis = jnp.concatenate([jnp.cos(angles), jnp.sin(angles)], axis=0)
    doubled = jnp.concatenate([response, response], axis=1)
    weighted = doubled[:, :, None] * basis[None]
    return jnp.einsum("rka,kb->rab", weighted, basis, precision=lax.Precision.HIGHEST) / cycle_size


def tangent_step(model_state, extend_rows, drift_coef, kernel):
    padded = extend_rows(model_state)
    north_row = padded[:, :, :-2]
    south_row = padded[:, :, 2:]
    east_cell = jnp.roll(model_state, -1, axis=3)
    west_cell = jnp.roll(model_state, 1, axis=3)
    updated = model_state + diffusion * (north_row + south_row + east_cell + west_cell - 4.0 * model_state) + drift_coef * (east_cell - west_cell)
    return jnp.einsum("flrb,rbc->flrc", updated, kernel, precision=lax.Precision.HIGHEST)


def adjoint_step(costate, extend_rows, drift_coef, kernel):
    filtered = jnp.einsum("flrb,rbc->flrc", costate, kernel, precision=lax.Precision.HIGHEST)
    padded = extend_rows(filtered)
    north_row = padded[:, :, :-2]
    south_row = padded[:, :, 2:]
    east_cell = jnp.roll(filtered, -1, axis=3)
    west_cell = jnp.roll(filtered, 1, axis=3)
    carried = drift_coef * filtered
    return filtered + diffusion * (north_row + south_row + east_cell + west_cell - 4.0 * filtered) + jnp.roll(carried, 1, axis=3) - jnp.roll(carried, -1, axis=3)


def pad_rows(model_state):
    return jnp.pad(model_state, ((0, 0), (0, 0), (1, 1), (0, 0)))


def reference(trajectory, innovation, background, obs_weight):
    coarse_rows = NLAT_C
    cycle_size = NLON_C
    zonal_wind = trajectory[0].astype(jnp.float32).reshape(LEVELS, coarse_rows, COARSEN, cycle_size, COARSEN)
    zonal_wind = jnp.mean(zonal_wind, axis=(2, 4))
    drift_coef = (advection_scale * jnp.tanh(zonal_wind))[None]
    kernel = filter_rows(jnp.arange(coarse_rows, dtype=jnp.int32), coarse_rows, cycle_size)
    increment = background
    for outer_turn in range(ITERS):
        model_state = increment
        for step_index in range(STEPS):
            model_state = tangent_step(model_state, pad_rows, drift_coef, kernel)
        costate = obs_weight[None] * (model_state - innovation)
        for step_index in range(STEPS):
            costate = adjoint_step(costate, pad_rows, drift_coef, kernel)
        increment = increment - descent_step * (increment - background + costate)

    def finish(field_pair):
        layer_field, coarse_part = field_pair
        fine_part = jnp.repeat(jnp.repeat(coarse_part, COARSEN, axis=2), COARSEN, axis=1)
        return (layer_field.astype(jnp.float32) + fine_part).astype(jnp.bfloat16)

    return lax.map(finish, (trajectory, increment))
```

```python
import functools

import jax
import jax.numpy as jnp
import numpy as np
from jax import lax
from jax.experimental import pallas as pl
from jax.experimental.pallas import tpu as pltpu
from jax.sharding import PartitionSpec as P

MESH = pl.DeviceIdType.MESH
FIELDS = 5
COARSEN = 4
STEPS = 2
LANES = 128
SUB = 8
HALO = 2 * STEPS
ITEMS = 2 * FIELDS + 2
PACKED = ITEMS // 4

diffusion = 0.2
advection_scale = 0.3
descent_step = 1.0


def split_bf16(x):
    high = x.astype(jnp.bfloat16)
    low = (x - high.astype(jnp.float32)).astype(jnp.bfloat16)
    return high, low


def dot(a, b):
    return jnp.dot(a, b, preferred_element_type=jnp.float32)


def block_transpose(tiles, block):
    lane = lax.broadcasted_iota(jnp.int32, tiles[0].shape, len(tiles[0].shape) - 1) // block
    axis = len(tiles[0].shape) - 1
    tiles = list(tiles)
    for step in (2, 1):
        upper = (lane // step) % 2 == 1
        for first in range(4):
            if (first // step) % 2 == 0:
                second = first + step
                a, b = tiles[first], tiles[second]
                tiles[first] = jnp.where(upper, pltpu.roll(b, step * block, axis), a)
                tiles[second] = jnp.where(upper, b, pltpu.roll(a, LANES - step * block, axis))
    return tiles


def stencil(q, drift):
    rows, cycle = q.shape[-2:]
    north = pltpu.roll(q, 1, q.ndim - 2)
    south = pltpu.roll(q, rows - 1, q.ndim - 2)
    east = pltpu.roll(q, cycle - 1, q.ndim - 1)
    west = pltpu.roll(q, 1, q.ndim - 1)
    return (
        (1.0 - 4.0 * diffusion) * q
        + diffusion * (north + south)
        + (diffusion + drift) * east
        + (diffusion - drift) * west
    )


def stencil_transposed(g, drift):
    rows, cycle = g.shape[-2:]
    north = pltpu.roll(g, 1, g.ndim - 2)
    south = pltpu.roll(g, rows - 1, g.ndim - 2)
    return (
        (1.0 - 4.0 * diffusion) * g
        + diffusion * (north + south)
        + pltpu.roll((diffusion + drift) * g, 1, g.ndim - 1)
        + pltpu.roll((diffusion - drift) * g, cycle - 1, g.ndim - 1)
    )


def chunk_sizes(levels):
    sizes = []
    left = levels
    while left:
        size = 3 if left > 3 else 2 if left == 3 else left
        sizes.append(size)
        left -= size
    return sizes


def analysis_kernel(
    wide_count, narrow_count, levels, chunks,
    traj_ref, depart_ref, back_ref, weight_ref, wave_ref, out_ref,
    depart, back, weight, wave, pool, spread, response, sums, sent, landed, fields, result,
    outgoing, returned, tall, up_out, down_out, up_in, down_in,
    load_sem, local_sem, send_sem, recv_sem, halo_send, halo_recv, back_send, back_recv,
):
    me = lax.axis_index("wide")
    band = lax.axis_index("narrow")
    has_above = band > 0
    has_below = band < narrow_count - 1
    total_levels = traj_ref.shape[1]
    fine_rows, fine_cols = traj_ref.shape[2:]
    halves = fine_rows // (SUB * COARSEN)
    rows = halves * SUB
    cycle = wave.shape[1]
    half = cycle // 2
    cols = cycle // wide_count
    padded = fields.shape[1]
    line = PACKED * SUB
    owners = -(-total_levels // levels)
    turns = len(chunks)
    starts = [sum(chunks[:t]) for t in range(turns)]
    ends = [starts[t] + chunks[t] for t in range(turns)]
    groups = outgoing.shape[1]
    group_ends = [groups if e == levels else FIELDS * e // 4 for e in ends]
    group_starts = [0] + group_ends[:-1]

    barrier = pltpu.get_barrier_semaphore()
    for k in range(1, wide_count):
        pl.semaphore_signal(
            barrier, inc=1, device_id=(lax.rem(me + k, wide_count), band), device_id_type=MESH
        )

    @pl.when(has_above)
    def _():
        pl.semaphore_signal(barrier, inc=1, device_id=(me, band - 1), device_id_type=MESH)

    @pl.when(has_below)
    def _():
        pl.semaphore_signal(barrier, inc=1, device_id=(me, band + 1), device_id_type=MESH)

    def loads(h):
        part = pl.ds(h * SUB, SUB)
        fine = pl.ds(h * SUB * COARSEN, SUB * COARSEN)
        pairs = [
            (back_ref.at[:, part], back.at[:, part]),
            (depart_ref.at[:, part], depart.at[:, part]),
            (weight_ref.at[part], weight.at[part]),
            (traj_ref.at[0, :, fine], out_ref.at[0, :, fine]),
        ]
        return [
            pltpu.make_async_copy(src, dst, load_sem.at[h, n]) for n, (src, dst) in enumerate(pairs)
        ]

    loading = [loads(h) for h in range(halves)]
    for h in range(halves):
        for copy in loading[h]:
            copy.start()
    load_wave = pltpu.make_async_copy(wave_ref, wave, local_sem.at[0])
    load_wave.start()
    load_rest = pltpu.make_async_copy(
        traj_ref.at[pl.ds(1, FIELDS - 1)], out_ref.at[pl.ds(1, FIELDS - 1)], local_sem.at[1]
    )

    lane = lax.broadcasted_iota(jnp.int32, (fine_cols, LANES), 1)
    source = lax.broadcasted_iota(jnp.int32, (fine_cols, LANES), 0)
    pool[...] = (lane == FIELDS % 4 * cols + source // COARSEN).astype(jnp.float32).astype(jnp.bfloat16)

    def item(index, row):
        if index < FIELDS:
            return back[index, row]
        if index < FIELDS + 2:
            return weight[row]
        return depart[index - FIELDS - 2, row]

    def pack(h):
        for n in range(3):
            loading[h][n].wait()
        for group in range(PACKED):
            for r in range(SUB):
                stacked = jnp.concatenate([item(4 * group + j, h * SUB + r) for j in range(4)], axis=0)
                sent[h, pl.ds(group * SUB + r, total_levels, stride=line), :] = stacked.T
        loading[h][3].wait()
        fine = out_ref[0, :, h * SUB * COARSEN : (h + 1) * SUB * COARSEN]
        count = total_levels * SUB
        sums[...] = dot(fine.reshape(count * COARSEN, fine_cols), pool[...])
        total = sums[pl.ds(0, count, stride=COARSEN), :]
        for t in range(1, COARSEN):
            total = total + sums[pl.ds(t, count, stride=COARSEN), :]
        drift = advection_scale * jnp.tanh(total * (1.0 / (COARSEN * COARSEN)))
        is_drift = lax.broadcasted_iota(jnp.int32, (SUB, LANES), 1) // cols == FIELDS % 4
        for level in range(total_levels):
            at = level * line + FIELDS // 4 * SUB
            sent[h, at : at + SUB] = jnp.where(
                is_drift, drift[level * SUB : (level + 1) * SUB], sent[h, at : at + SUB]
            )

    sends = {}

    def send(turn, h):
        size = chunks[turn] * line
        for k in range(1, wide_count):
            peer = lax.rem(me + k, wide_count)
            copy = pltpu.make_async_remote_copy(
                src_ref=sent.at[h, pl.ds(peer * (levels * line) + starts[turn] * line, size)],
                dst_ref=landed.at[me, h, pl.ds(starts[turn] * line, size)],
                send_sem=send_sem.at[turn, h, k],
                recv_sem=recv_sem.at[turn, h, k],
                device_id=(peer, band),
                device_id_type=MESH,
            )
            copy.start()
            sends[turn, h, k] = copy

    pack(0)
    neighbours = has_above.astype(jnp.int32) + has_below.astype(jnp.int32)
    pl.semaphore_wait(barrier, wide_count - 1 + neighbours)
    send(0, 0)
    for h in range(1, halves):
        pack(h)
        send(0, h)
    for turn in range(1, turns):
        for h in range(halves):
            send(turn, h)
    keeps = [
        pltpu.make_async_copy(
            sent.at[h, pl.ds(me * (levels * line), levels * line)], landed.at[me, h], local_sem.at[2 + h]
        )
        for h in range(halves)
    ]
    for copy in keeps:
        copy.start()
    load_rest.start()

    place = lax.broadcasted_iota(jnp.int32, (padded, cycle), 0)
    row_index = jnp.where(place < rows + HALO, place, place - padded) + band * rows
    wavenumber = lax.broadcasted_iota(jnp.int32, (padded, cycle), 1)
    folded = jnp.minimum(wavenumber, cycle - wavenumber).astype(jnp.float32)
    total_rows = rows * narrow_count
    latitude = jnp.pi * ((row_index.astype(jnp.float32) + 0.5) / total_rows - 0.5)
    inside = (row_index >= 0) & (row_index < total_rows)
    cutoff = jnp.where(inside, 0.5 * cycle * jnp.cos(latitude), 1.0)
    squared = (folded / cutoff) * (folded / cutoff)
    response[...] = jnp.where(inside, 1.0 / (1.0 + squared * squared), 0.0) / cycle

    source = lax.broadcasted_iota(jnp.int32, spread.shape, 0) % LANES
    lane = lax.broadcasted_iota(jnp.int32, spread.shape, 1)
    spread[...] = (
        (source == lane // LANES * cols + lane % LANES // COARSEN).astype(jnp.float32).astype(jnp.bfloat16)
    )

    @pl.when(jnp.logical_not(has_below))
    def _():
        up_in[...] = jnp.zeros_like(up_in)

    @pl.when(jnp.logical_not(has_above))
    def _():
        down_in[...] = jnp.zeros_like(down_in)

    for copy in keeps:
        copy.wait()

    low_half = lax.broadcasted_iota(jnp.int32, (SUB, half), 0) < HALO

    def unpack(level, carry):
        for group in range(PACKED):
            at = pl.ds(pl.multiple_of(level * line + group * SUB, SUB), SUB)
            for tile in range(cycle // LANES):
                for h in range(halves):
                    got = [landed[4 * tile + m, h, at] for m in range(4)]
                    for j, value in enumerate(block_transpose(got, cols)):
                        fields[
                            level * ITEMS + 4 * group + j,
                            h * SUB : (h + 1) * SUB,
                            tile * LANES : (tile + 1) * LANES,
                        ] = value
        for index in range(ITEMS):
            at = level * ITEMS + index
            top = fields[at, 0:SUB]
            bottom = fields[at, rows - SUB : rows]
            up_out[at] = jnp.where(low_half, top[:, :half], pltpu.roll(top[:, half:], HALO, 0))
            down_out[at] = jnp.where(low_half, pltpu.roll(bottom[:, :half], HALO, 0), bottom[:, half:])
        return carry

    def halo_copies(turn):
        part = pl.ds(starts[turn] * ITEMS, chunks[turn] * ITEMS)
        up_copy = pltpu.make_async_remote_copy(
            src_ref=up_out.at[part], dst_ref=up_in.at[part],
            send_sem=halo_send.at[turn, 0], recv_sem=halo_recv.at[turn, 0],
            device_id=(me, band - 1), device_id_type=MESH,
        )
        down_copy = pltpu.make_async_remote_copy(
            src_ref=down_out.at[part], dst_ref=down_in.at[part],
            send_sem=halo_send.at[turn, 1], recv_sem=halo_recv.at[turn, 1],
            device_id=(me, band + 1), device_id_type=MESH,
        )
        return up_copy, down_copy

    def take_halo(level, carry):
        for index in range(ITEMS):
            at = level * ITEMS + index
            below, above = up_in[at], down_in[at]
            fields[at, rows:padded, 0:half] = jnp.where(low_half, below, pltpu.roll(above, HALO, 0))
            fields[at, rows:padded, half:cycle] = jnp.where(low_half, pltpu.roll(below, HALO, 0), above)
        return carry

    def transform(q):
        count = q.shape[0]
        high, low = split_bf16(q)
        wave_high, wave_low = wave[0:cycle], wave[cycle : 2 * cycle]
        both = dot(jnp.concatenate([high, low], axis=0), wave_high)
        return both[:count] + both[count:] + dot(high, wave_low)

    def zonal(q):
        shape = q.shape
        spectrum = transform(q.reshape(-1, cycle)).reshape(shape) * response[...]
        return transform(spectrum.reshape(-1, cycle)).reshape(shape)

    def sweep(turn):
        at, chunk = starts[turn], chunks[turn]
        block = fields[at * ITEMS : (at + chunk) * ITEMS].reshape(chunk, ITEMS, padded, cycle)
        background = block[:, :FIELDS]
        drift = block[:, FIELDS : FIELDS + 1]
        observed = block[:, FIELDS + 1 : FIELDS + 2]
        departure = block[:, FIELDS + 2 :]
        state = background
        for _ in range(STEPS):
            state = zonal(stencil(state, drift))
        costate = observed * (state - departure)
        for _ in range(STEPS):
            costate = stencil_transposed(zonal(costate), drift)
        increment = background - descent_step * ((background - background) + costate)
        result[at * FIELDS : (at + chunk) * FIELDS] = increment.reshape(chunk * FIELDS, padded, cycle)[:, :rows]

    def repack(group, carry):
        for tile in range(cycle // LANES):
            parts = [result[4 * group + j, :, tile * LANES : (tile + 1) * LANES] for j in range(4)]
            for m, value in enumerate(block_transpose(parts, cols)):
                outgoing[4 * tile + m, group] = value
        return carry

    backs = {}

    def receive(turn):
        for h in range(halves):
            for k in range(1, wide_count):
                sends[turn, h, k].wait_recv()
        lax.fori_loop(starts[turn], ends[turn], unpack, 0)
        up_copy, down_copy = halo_copies(turn)

        @pl.when(has_above)
        def _():
            up_copy.start()

        @pl.when(has_below)
        def _():
            down_copy.start()

    def compute(turn):
        up_copy, down_copy = halo_copies(turn)

        @pl.when(has_below)
        def _():
            up_copy.wait_recv()

        @pl.when(has_above)
        def _():
            down_copy.wait_recv()

        lax.fori_loop(starts[turn], ends[turn], take_halo, 0)
        sweep(turn)
        first, end = group_starts[turn], group_ends[turn]
        lax.fori_loop(first, end, repack, 0)
        part = pl.ds(first, end - first)
        keep_back = pltpu.make_async_copy(
            outgoing.at[me, part], returned.at[me, part], back_send.at[turn, 0]
        )
        keep_back.start()
        backs[turn, 0] = keep_back
        for k in range(1, wide_count):
            peer = lax.rem(me + k, wide_count)
            copy = pltpu.make_async_remote_copy(
                src_ref=outgoing.at[peer, part],
                dst_ref=returned.at[me, part],
                send_sem=back_send.at[turn, k],
                recv_sem=back_recv.at[turn, k],
                device_id=(peer, band),
                device_id_type=MESH,
            )
            copy.start()
            backs[turn, k] = copy

    def finish(turn):
        first, end = group_starts[turn], group_ends[turn]
        count = end - first
        span = count * rows
        backs[turn, 0].wait()
        for k in range(1, wide_count):
            backs[turn, k].wait_recv()

        def owner(s, carry):
            part = returned[s, first:end].reshape(span, LANES)
            for t in range(COARSEN):
                tall[pl.ds(t, span, stride=COARSEN), :] = part
            operand = jnp.concatenate(split_bf16(tall[0 : span * COARSEN]), axis=1)
            wide = dot(operand, spread[...])

            def put(group, j, place):
                f = place % FIELDS
                level = s * levels + place // FIELDS
                fine = wide[group * fine_rows : (group + 1) * fine_rows, j * LANES : j * LANES + fine_cols]
                out_ref[f, level] = (out_ref[f, level].astype(jnp.float32) + fine).astype(jnp.bfloat16)

            for group in range(count):
                for j in range(4):
                    place = 4 * (first + group) + j
                    if place < levels * FIELDS:
                        if owners * levels == total_levels:
                            put(group, j, place)
                        else:
                            pl.when(s * levels + place // FIELDS < total_levels)(
                                functools.partial(put, group, j, place)
                            )
            return carry

        lax.fori_loop(0, owners, owner, 0)

    load_wave.wait()
    for turn in range(turns):
        receive(turn)
        if turn > 0:
            compute(turn - 1)
    compute(turns - 1)
    load_rest.wait()
    for turn in range(turns):
        finish(turn)

    for copy in sends.values():
        copy.wait_send()
    for turn in range(turns):
        up_copy, down_copy = halo_copies(turn)

        @pl.when(has_above)
        def _():
            up_copy.wait_send()

        @pl.when(has_below)
        def _():
            down_copy.wait_send()

        for k in range(1, wide_count):
            backs[turn, k].wait_send()


def shards(trajectory, innovation, background, obs_weight):
    wide_count = lax.axis_size("wide")
    narrow_count = lax.axis_size("narrow")
    fields, total_levels, rows, cols = innovation.shape
    fine_rows, fine_cols = trajectory.shape[2:]
    cycle = cols * wide_count
    levels = -(-total_levels // wide_count)
    chunks = chunk_sizes(levels)
    turns = len(chunks)
    groups = -(-fields * levels // 4)
    padded = rows + 2 * HALO
    halves = rows // SUB
    line = PACKED * SUB

    phase = np.arange(cycle)[:, None] * np.arange(cycle)[None, :] % cycle
    wave = np.cos(2.0 * np.pi / cycle * phase) + np.sin(2.0 * np.pi / cycle * phase)
    wave = wave.astype(np.float32)
    wave_high = wave.astype(jnp.bfloat16)
    wave_low = (wave - wave_high.astype(np.float32)).astype(jnp.bfloat16)
    wave = jnp.asarray(np.concatenate([wave_high, wave_low]))

    hbm = pl.BlockSpec(memory_space=pltpu.HBM)
    vmem = pl.BlockSpec(memory_space=pltpu.VMEM)
    f32 = jnp.float32
    bf16 = jnp.bfloat16
    dma = pltpu.SemaphoreType.DMA
    return pl.pallas_call(
        functools.partial(analysis_kernel, wide_count, narrow_count, levels, chunks),
        in_specs=[hbm] * 5,
        out_specs=vmem,
        out_shape=pltpu.VMEM(trajectory.shape, bf16),
        scratch_shapes=[
            pltpu.VMEM((fields, rows, cols, total_levels), f32),
            pltpu.VMEM((fields, rows, cols, total_levels), f32),
            pltpu.VMEM((rows, cols, total_levels), f32),
            pltpu.VMEM((2 * cycle, cycle), bf16),
            pltpu.VMEM((fine_cols, LANES), bf16),
            pltpu.VMEM((2 * LANES, 4 * LANES), bf16),
            pltpu.VMEM((padded, cycle), f32),
            pltpu.VMEM((total_levels * SUB * COARSEN, LANES), f32),
            pltpu.VMEM((halves, wide_count * levels * line, LANES), f32),
            pltpu.VMEM((wide_count, halves, levels * line, LANES), f32),
            pltpu.VMEM((levels * ITEMS, padded, cycle), f32),
            pltpu.VMEM((groups * 4, rows, cycle), f32),
            pltpu.VMEM((wide_count, groups, rows, LANES), f32),
            pltpu.VMEM((wide_count, groups, rows, LANES), f32),
            pltpu.VMEM((groups * fine_rows, LANES), f32),
            pltpu.VMEM((levels * ITEMS, SUB, cycle // 2), f32),
            pltpu.VMEM((levels * ITEMS, SUB, cycle // 2), f32),
            pltpu.VMEM((levels * ITEMS, SUB, cycle // 2), f32),
            pltpu.VMEM((levels * ITEMS, SUB, cycle // 2), f32),
            dma((halves, 4)),
            dma((2 + halves,)),
            dma((turns, halves, wide_count)),
            dma((turns, halves, wide_count)),
            dma((turns, 2)),
            dma((turns, 2)),
            dma((turns, wide_count)),
            dma((turns, wide_count)),
        ],
        compiler_params=pltpu.CompilerParams(
            collective_id=0, has_side_effects=True, vmem_limit_bytes=40 * 1024 * 1024
        ),
        name="analysis",
    )(
        *(
            pltpu.with_memory_space_constraint(x, pltpu.HBM)
            for x in (
                trajectory,
                innovation.transpose(0, 2, 3, 1),
                background.transpose(0, 2, 3, 1),
                obs_weight.transpose(1, 2, 0),
                wave,
            )
        )
    )


def solution(mesh):
    in_specs = (
        P(None, None, "narrow", "wide"),
        P(None, None, "narrow", "wide"),
        P(None, None, "narrow", "wide"),
        P(None, "narrow", "wide"),
    )
    out_specs = P(None, None, "narrow", "wide")
    return jax.shard_map(shards, mesh=mesh, in_specs=in_specs, out_specs=out_specs, check_vma=False)
```

```python
import functools

import jax
import jax.numpy as jnp
import numpy as np
from jax import lax
from jax.experimental import pallas as pl
from jax.experimental.pallas import tpu as pltpu
from jax.sharding import PartitionSpec as P

MESH = pl.DeviceIdType.MESH
FIELDS = 5
COARSEN = 4
STEPS = 2
LANES = 128
SUB = 8
HALO = 2 * STEPS
ITEMS = 2 * FIELDS + 2
PACKED = ITEMS // 4

diffusion = 0.2
advection_scale = 0.3
descent_step = 1.0


def split_bf16(x):
    high = x.astype(jnp.bfloat16)
    low = (x - high.astype(jnp.float32)).astype(jnp.bfloat16)
    return high, low


def dot(a, b):
    return jnp.dot(a, b, preferred_element_type=jnp.float32)


def block_transpose(tiles, block):
    lane = lax.broadcasted_iota(jnp.int32, tiles[0].shape, len(tiles[0].shape) - 1) // block
    axis = len(tiles[0].shape) - 1
    tiles = list(tiles)
    for step in (2, 1):
        upper = (lane // step) % 2 == 1
        for first in range(4):
            if (first // step) % 2 == 0:
                second = first + step
                a, b = tiles[first], tiles[second]
                tiles[first] = jnp.where(upper, pltpu.roll(b, step * block, axis), a)
                tiles[second] = jnp.where(upper, b, pltpu.roll(a, LANES - step * block, axis))
    return tiles


def stencil(q, drift):
    rows, cycle = q.shape[-2:]
    north = pltpu.roll(q, 1, q.ndim - 2)
    south = pltpu.roll(q, rows - 1, q.ndim - 2)
    east = pltpu.roll(q, cycle - 1, q.ndim - 1)
    west = pltpu.roll(q, 1, q.ndim - 1)
    return (
        (1.0 - 4.0 * diffusion) * q
        + diffusion * (north + south)
        + (diffusion + drift) * east
        + (diffusion - drift) * west
    )


def stencil_transposed(g, drift):
    rows, cycle = g.shape[-2:]
    north = pltpu.roll(g, 1, g.ndim - 2)
    south = pltpu.roll(g, rows - 1, g.ndim - 2)
    return (
        (1.0 - 4.0 * diffusion) * g
        + diffusion * (north + south)
        + pltpu.roll((diffusion + drift) * g, 1, g.ndim - 1)
        + pltpu.roll((diffusion - drift) * g, cycle - 1, g.ndim - 1)
    )


def chunk_sizes(levels):
    return [2] * (levels // 2) + [1] * (levels % 2)


def complete_groups(chunks):
    levels = sum(chunks)
    ends = [sum(chunks[: t + 1]) for t in range(len(chunks))]
    return [0] + [-(-FIELDS * e // 4) if e == levels else FIELDS * e // 4 for e in ends]


def analysis_kernel(
    wide_count, narrow_count, levels, chunks,
    traj_ref, depart_ref, back_ref, weight_ref, wave_ref, out_ref,
    depart, back, weight, wave, pool, spread, response, sums, sent, landed, fields, result,
    outgoing, returned, tall, up_out, down_out, up_in, down_in,
    load_sem, local_sem, send_sem, recv_sem, halo_send, halo_recv, back_send, back_recv,
):
    me = lax.axis_index("wide")
    band = lax.axis_index("narrow")
    has_above = band > 0
    has_below = band < narrow_count - 1
    total_levels = traj_ref.shape[1]
    fine_rows, fine_cols = traj_ref.shape[2:]
    halves = fine_rows // (SUB * COARSEN)
    rows = halves * SUB
    cycle = wave.shape[1]
    half = cycle // 2
    cols = cycle // wide_count
    padded = fields.shape[1]
    line = PACKED * SUB
    owners = -(-total_levels // levels)
    turns = len(chunks)
    starts = [sum(chunks[:t]) for t in range(turns)]
    ends = [starts[t] + chunks[t] for t in range(turns)]
    group_bounds = complete_groups(chunks)

    barrier = pltpu.get_barrier_semaphore()
    for k in range(1, wide_count):
        pl.semaphore_signal(
            barrier, inc=1, device_id=(lax.rem(me + k, wide_count), band), device_id_type=MESH
        )

    @pl.when(has_above)
    def _():
        pl.semaphore_signal(barrier, inc=1, device_id=(me, band - 1), device_id_type=MESH)

    @pl.when(has_below)
    def _():
        pl.semaphore_signal(barrier, inc=1, device_id=(me, band + 1), device_id_type=MESH)

    def loads(h):
        part = pl.ds(h * SUB, SUB)
        fine = pl.ds(h * SUB * COARSEN, SUB * COARSEN)
        pairs = [
            (back_ref.at[:, part], back.at[:, part]),
            (depart_ref.at[:, part], depart.at[:, part]),
            (weight_ref.at[part], weight.at[part]),
            (traj_ref.at[0, :, fine], out_ref.at[0, :, fine]),
        ]
        return [
            pltpu.make_async_copy(src, dst, load_sem.at[h, n]) for n, (src, dst) in enumerate(pairs)
        ]

    loading = [loads(h) for h in range(halves)]
    for h in range(halves):
        for copy in loading[h]:
            copy.start()
    load_wave = pltpu.make_async_copy(wave_ref, wave, local_sem.at[0])
    load_wave.start()
    load_rest = pltpu.make_async_copy(
        traj_ref.at[pl.ds(1, FIELDS - 1)], out_ref.at[pl.ds(1, FIELDS - 1)], local_sem.at[1]
    )

    lane = lax.broadcasted_iota(jnp.int32, (fine_cols, LANES), 1)
    source = lax.broadcasted_iota(jnp.int32, (fine_cols, LANES), 0)
    pool[...] = (lane == FIELDS % 4 * cols + source // COARSEN).astype(jnp.float32).astype(jnp.bfloat16)

    def item(index, row):
        if index < FIELDS:
            return back[index, row]
        if index < FIELDS + 2:
            return weight[row]
        return depart[index - FIELDS - 2, row]

    def pack(h):
        for n in range(3):
            loading[h][n].wait()
        for group in range(PACKED):
            for r in range(SUB):
                stacked = jnp.concatenate([item(4 * group + j, h * SUB + r) for j in range(4)], axis=0)
                sent[h, pl.ds(group * SUB + r, total_levels, stride=line), :] = stacked.T
        loading[h][3].wait()
        fine = out_ref[0, :, h * SUB * COARSEN : (h + 1) * SUB * COARSEN]
        count = total_levels * SUB
        sums[...] = dot(fine.reshape(count * COARSEN, fine_cols), pool[...])
        total = sums[pl.ds(0, count, stride=COARSEN), :]
        for t in range(1, COARSEN):
            total = total + sums[pl.ds(t, count, stride=COARSEN), :]
        drift = advection_scale * jnp.tanh(total * (1.0 / (COARSEN * COARSEN)))
        is_drift = lax.broadcasted_iota(jnp.int32, (SUB, LANES), 1) // cols == FIELDS % 4
        for level in range(total_levels):
            at = level * line + FIELDS // 4 * SUB
            sent[h, at : at + SUB] = jnp.where(
                is_drift, drift[level * SUB : (level + 1) * SUB], sent[h, at : at + SUB]
            )

    sends = {}

    def send(turn, h):
        size = chunks[turn] * line
        for k in range(1, wide_count):
            peer = lax.rem(me + k, wide_count)
            copy = pltpu.make_async_remote_copy(
                src_ref=sent.at[h, pl.ds(peer * (levels * line) + starts[turn] * line, size)],
                dst_ref=landed.at[me, h, pl.ds(starts[turn] * line, size)],
                send_sem=send_sem.at[turn, h, k],
                recv_sem=recv_sem.at[turn, h, k],
                device_id=(peer, band),
                device_id_type=MESH,
            )
            copy.start()
            sends[turn, h, k] = copy

    pack(0)
    neighbours = has_above.astype(jnp.int32) + has_below.astype(jnp.int32)
    pl.semaphore_wait(barrier, wide_count - 1 + neighbours)
    send(0, 0)
    for h in range(1, halves):
        pack(h)
        send(0, h)
    for turn in range(1, turns):
        for h in range(halves):
            send(turn, h)
    keeps = [
        pltpu.make_async_copy(
            sent.at[h, pl.ds(me * (levels * line), levels * line)], landed.at[me, h], local_sem.at[2 + h]
        )
        for h in range(halves)
    ]
    for copy in keeps:
        copy.start()
    load_rest.start()

    place = lax.broadcasted_iota(jnp.int32, (padded, cycle), 0)
    row_index = jnp.where(place < rows + HALO, place, place - padded) + band * rows
    wavenumber = lax.broadcasted_iota(jnp.int32, (padded, cycle), 1)
    folded = jnp.minimum(wavenumber, cycle - wavenumber).astype(jnp.float32)
    total_rows = rows * narrow_count
    latitude = jnp.pi * ((row_index.astype(jnp.float32) + 0.5) / total_rows - 0.5)
    inside = (row_index >= 0) & (row_index < total_rows)
    cutoff = jnp.where(inside, 0.5 * cycle * jnp.cos(latitude), 1.0)
    squared = (folded / cutoff) * (folded / cutoff)
    response[...] = jnp.where(inside, 1.0 / (1.0 + squared * squared), 0.0) / cycle

    source = lax.broadcasted_iota(jnp.int32, spread.shape, 0) % LANES
    lane = lax.broadcasted_iota(jnp.int32, spread.shape, 1)
    spread[...] = (
        (source == lane // LANES * cols + lane % LANES // COARSEN).astype(jnp.float32).astype(jnp.bfloat16)
    )

    @pl.when(jnp.logical_not(has_below))
    def _():
        up_in[...] = jnp.zeros_like(up_in)

    @pl.when(jnp.logical_not(has_above))
    def _():
        down_in[...] = jnp.zeros_like(down_in)

    for copy in keeps:
        copy.wait()

    low_half = lax.broadcasted_iota(jnp.int32, (SUB, half), 0) < HALO

    def unpack(level):
        for group in range(PACKED):
            at = pl.ds(level * line + group * SUB, SUB)
            for tile in range(cycle // LANES):
                for h in range(halves):
                    got = [landed[4 * tile + m, h, at] for m in range(4)]
                    for j, value in enumerate(block_transpose(got, cols)):
                        fields[
                            level * ITEMS + 4 * group + j,
                            h * SUB : (h + 1) * SUB,
                            tile * LANES : (tile + 1) * LANES,
                        ] = value
        for index in range(ITEMS):
            at = level * ITEMS + index
            top = fields[at, 0:SUB]
            bottom = fields[at, rows - SUB : rows]
            up_out[at] = jnp.where(low_half, top[:, :half], pltpu.roll(top[:, half:], HALO, 0))
            down_out[at] = jnp.where(low_half, pltpu.roll(bottom[:, :half], HALO, 0), bottom[:, half:])

    def halo_copies(turn):
        part = pl.ds(starts[turn] * ITEMS, chunks[turn] * ITEMS)
        up_copy = pltpu.make_async_remote_copy(
            src_ref=up_out.at[part], dst_ref=up_in.at[part],
            send_sem=halo_send.at[turn, 0], recv_sem=halo_recv.at[turn, 0],
            device_id=(me, band - 1), device_id_type=MESH,
        )
        down_copy = pltpu.make_async_remote_copy(
            src_ref=down_out.at[part], dst_ref=down_in.at[part],
            send_sem=halo_send.at[turn, 1], recv_sem=halo_recv.at[turn, 1],
            device_id=(me, band + 1), device_id_type=MESH,
        )
        return up_copy, down_copy

    def take_halo(level):
        for index in range(ITEMS):
            at = level * ITEMS + index
            below, above = up_in[at], down_in[at]
            fields[at, rows:padded, 0:half] = jnp.where(low_half, below, pltpu.roll(above, HALO, 0))
            fields[at, rows:padded, half:cycle] = jnp.where(low_half, pltpu.roll(below, HALO, 0), above)

    def transform(q):
        count = q.shape[0]
        high, low = split_bf16(q)
        wave_high, wave_low = wave[0:cycle], wave[cycle : 2 * cycle]
        both = dot(jnp.concatenate([high, low], axis=0), wave_high)
        return both[:count] + both[count:] + dot(high, wave_low)

    def zonal(q):
        shape = q.shape
        spectrum = transform(q.reshape(-1, cycle)).reshape(shape) * response[...]
        return transform(spectrum.reshape(-1, cycle)).reshape(shape)

    def sweep(turn):
        at, chunk = starts[turn], chunks[turn]
        block = fields[at * ITEMS : (at + chunk) * ITEMS].reshape(chunk, ITEMS, padded, cycle)
        background = block[:, :FIELDS]
        drift = block[:, FIELDS : FIELDS + 1]
        observed = block[:, FIELDS + 1 : FIELDS + 2]
        departure = block[:, FIELDS + 2 :]
        state = background
        for _ in range(STEPS):
            state = zonal(stencil(state, drift))
        costate = observed * (state - departure)
        for _ in range(STEPS):
            costate = stencil_transposed(zonal(costate), drift)
        increment = background - descent_step * ((background - background) + costate)
        result[at * FIELDS : (at + chunk) * FIELDS] = increment.reshape(chunk * FIELDS, padded, cycle)[:, :rows]

    def repack(group):
        for tile in range(cycle // LANES):
            parts = [result[4 * group + j, :, tile * LANES : (tile + 1) * LANES] for j in range(4)]
            for m, value in enumerate(block_transpose(parts, cols)):
                outgoing[4 * tile + m, group] = value

    backs = {}

    def receive(turn):
        for h in range(halves):
            for k in range(1, wide_count):
                sends[turn, h, k].wait_recv()
        for level in range(starts[turn], ends[turn]):
            unpack(level)
        up_copy, down_copy = halo_copies(turn)

        @pl.when(has_above)
        def _():
            up_copy.start()

        @pl.when(has_below)
        def _():
            down_copy.start()

    def compute(turn):
        up_copy, down_copy = halo_copies(turn)

        @pl.when(has_below)
        def _():
            up_copy.wait_recv()

        @pl.when(has_above)
        def _():
            down_copy.wait_recv()

        for level in range(starts[turn], ends[turn]):
            take_halo(level)
        sweep(turn)
        first, end = group_bounds[turn : turn + 2]
        for group in range(first, end):
            repack(group)
        part = pl.ds(first, end - first)
        keep_back = pltpu.make_async_copy(
            outgoing.at[me, part], returned.at[me, part], back_send.at[turn, 0]
        )
        keep_back.start()
        backs[turn, 0] = keep_back
        for k in range(1, wide_count):
            peer = lax.rem(me + k, wide_count)
            copy = pltpu.make_async_remote_copy(
                src_ref=outgoing.at[peer, part],
                dst_ref=returned.at[me, part],
                send_sem=back_send.at[turn, k],
                recv_sem=back_recv.at[turn, k],
                device_id=(peer, band),
                device_id_type=MESH,
            )
            copy.start()
            backs[turn, k] = copy

    def finish(turn):
        first, end = group_bounds[turn : turn + 2]
        count = end - first
        span = count * rows
        backs[turn, 0].wait()
        for k in range(1, wide_count):
            backs[turn, k].wait_recv()

        def owner(s):
            part = returned[s, first:end].reshape(span, LANES)
            for t in range(COARSEN):
                tall[s, pl.ds(t, span, stride=COARSEN), :] = part
            operand = jnp.concatenate(split_bf16(tall[s, 0 : span * COARSEN]), axis=1)
            wide = dot(operand, spread[...])

            def put(group, j, place):
                f = place % FIELDS
                level = s * levels + place // FIELDS
                fine = wide[group * fine_rows : (group + 1) * fine_rows, j * LANES : j * LANES + fine_cols]
                out_ref[f, level] = (out_ref[f, level].astype(jnp.float32) + fine).astype(jnp.bfloat16)

            for group in range(count):
                for j in range(4):
                    place = 4 * (first + group) + j
                    if place < levels * FIELDS and s * levels + place // FIELDS < total_levels:
                        put(group, j, place)

        for s in range(owners):
            owner(s)

    load_wave.wait()
    for turn in range(turns):
        receive(turn)
        if turn > 0:
            compute(turn - 1)
    compute(turns - 1)
    load_rest.wait()
    for turn in range(turns):
        finish(turn)

    for copy in sends.values():
        copy.wait_send()
    for turn in range(turns):
        up_copy, down_copy = halo_copies(turn)

        @pl.when(has_above)
        def _():
            up_copy.wait_send()

        @pl.when(has_below)
        def _():
            down_copy.wait_send()

        for k in range(1, wide_count):
            backs[turn, k].wait_send()


def shards(trajectory, innovation, background, obs_weight):
    wide_count = lax.axis_size("wide")
    narrow_count = lax.axis_size("narrow")
    fields, total_levels, rows, cols = innovation.shape
    fine_rows, fine_cols = trajectory.shape[2:]
    cycle = cols * wide_count
    levels = -(-total_levels // wide_count)
    chunks = chunk_sizes(levels)
    turns = len(chunks)
    bounds = complete_groups(chunks)
    groups = bounds[-1]
    largest = max(end - first for first, end in zip(bounds, bounds[1:]))
    padded = rows + 2 * HALO
    halves = rows // SUB
    line = PACKED * SUB

    phase = np.arange(cycle)[:, None] * np.arange(cycle)[None, :] % cycle
    wave = np.cos(2.0 * np.pi / cycle * phase) + np.sin(2.0 * np.pi / cycle * phase)
    wave = wave.astype(np.float32)
    wave_high = wave.astype(jnp.bfloat16)
    wave_low = (wave - wave_high.astype(np.float32)).astype(jnp.bfloat16)
    wave = jnp.asarray(np.concatenate([wave_high, wave_low]))

    hbm = pl.BlockSpec(memory_space=pltpu.HBM)
    vmem = pl.BlockSpec(memory_space=pltpu.VMEM)
    f32 = jnp.float32
    bf16 = jnp.bfloat16
    dma = pltpu.SemaphoreType.DMA
    return pl.pallas_call(
        functools.partial(analysis_kernel, wide_count, narrow_count, levels, chunks),
        in_specs=[hbm] * 5,
        out_specs=vmem,
        out_shape=pltpu.VMEM(trajectory.shape, bf16),
        scratch_shapes=[
            pltpu.VMEM((fields, rows, cols, total_levels), f32),
            pltpu.VMEM((fields, rows, cols, total_levels), f32),
            pltpu.VMEM((rows, cols, total_levels), f32),
            pltpu.VMEM((2 * cycle, cycle), bf16),
            pltpu.VMEM((fine_cols, LANES), bf16),
            pltpu.VMEM((2 * LANES, 4 * LANES), bf16),
            pltpu.VMEM((padded, cycle), f32),
            pltpu.VMEM((total_levels * SUB * COARSEN, LANES), f32),
            pltpu.VMEM((halves, wide_count * levels * line, LANES), f32),
            pltpu.VMEM((wide_count, halves, levels * line, LANES), f32),
            pltpu.VMEM((levels * ITEMS, padded, cycle), f32),
            pltpu.VMEM((groups * 4, rows, cycle), f32),
            pltpu.VMEM((wide_count, groups, rows, LANES), f32),
            pltpu.VMEM((wide_count, groups, rows, LANES), f32),
            pltpu.VMEM((wide_count, largest * fine_rows, LANES), f32),
            pltpu.VMEM((levels * ITEMS, SUB, cycle // 2), f32),
            pltpu.VMEM((levels * ITEMS, SUB, cycle // 2), f32),
            pltpu.VMEM((levels * ITEMS, SUB, cycle // 2), f32),
            pltpu.VMEM((levels * ITEMS, SUB, cycle // 2), f32),
            dma((halves, 4)),
            dma((2 + halves,)),
            dma((turns, halves, wide_count)),
            dma((turns, halves, wide_count)),
            dma((turns, 2)),
            dma((turns, 2)),
            dma((turns, wide_count)),
            dma((turns, wide_count)),
        ],
        compiler_params=pltpu.CompilerParams(
            collective_id=0, has_side_effects=True, vmem_limit_bytes=40 * 1024 * 1024
        ),
        name="analysis",
    )(
        *(
            pltpu.with_memory_space_constraint(x, pltpu.HBM)
            for x in (
                trajectory,
                innovation.transpose(0, 2, 3, 1),
                background.transpose(0, 2, 3, 1),
                obs_weight.transpose(1, 2, 0),
                wave,
            )
        )
    )


def solution(mesh):
    in_specs = (
        P(None, None, "narrow", "wide"),
        P(None, None, "narrow", "wide"),
        P(None, None, "narrow", "wide"),
        P(None, "narrow", "wide"),
    )
    out_specs = P(None, None, "narrow", "wide")
    return jax.shard_map(shards, mesh=mesh, in_specs=in_specs, out_specs=out_specs, check_vma=False)
```

```python
import functools

import jax
import jax.numpy as jnp
import numpy as np
from jax import lax
from jax.experimental import pallas as pl
from jax.experimental.pallas import tpu as pltpu
from jax.sharding import PartitionSpec as P

MESH = pl.DeviceIdType.MESH
FIELDS = 5
COARSEN = 4
STEPS = 2
LANES = 128
SUB = 8
HALO = 2 * STEPS
ITEMS = 2 * FIELDS + 2
PACKED = ITEMS // 4

diffusion = 0.2
advection_scale = 0.3
descent_step = 1.0


def split_bf16(x):
    high = x.astype(jnp.bfloat16)
    low = (x - high.astype(jnp.float32)).astype(jnp.bfloat16)
    return high, low


def dot(a, b):
    return jnp.dot(a, b, preferred_element_type=jnp.float32)


def block_transpose(tiles, block):
    lane = lax.broadcasted_iota(jnp.int32, tiles[0].shape, len(tiles[0].shape) - 1) // block
    axis = len(tiles[0].shape) - 1
    tiles = list(tiles)
    for step in (2, 1):
        upper = (lane // step) % 2 == 1
        for first in range(4):
            if (first // step) % 2 == 0:
                second = first + step
                a, b = tiles[first], tiles[second]
                tiles[first] = jnp.where(upper, pltpu.roll(b, step * block, axis), a)
                tiles[second] = jnp.where(upper, b, pltpu.roll(a, LANES - step * block, axis))
    return tiles


def stencil(q, drift):
    rows, cycle = q.shape[-2:]
    north = pltpu.roll(q, 1, q.ndim - 2)
    south = pltpu.roll(q, rows - 1, q.ndim - 2)
    east = pltpu.roll(q, cycle - 1, q.ndim - 1)
    west = pltpu.roll(q, 1, q.ndim - 1)
    return (
        (1.0 - 4.0 * diffusion) * q
        + diffusion * (north + south)
        + (diffusion + drift) * east
        + (diffusion - drift) * west
    )


def stencil_transposed(g, drift):
    rows, cycle = g.shape[-2:]
    north = pltpu.roll(g, 1, g.ndim - 2)
    south = pltpu.roll(g, rows - 1, g.ndim - 2)
    return (
        (1.0 - 4.0 * diffusion) * g
        + diffusion * (north + south)
        + pltpu.roll((diffusion + drift) * g, 1, g.ndim - 1)
        + pltpu.roll((diffusion - drift) * g, cycle - 1, g.ndim - 1)
    )


def chunk_sizes(levels):
    if levels < 6:
        return [1] + [2] * ((levels - 1) // 2) + [1] * ((levels - 1) % 2)
    middle = levels - 6
    return [1, 2] + [3] * (middle // 3) + [middle % 3] * (middle % 3 > 0) + [2, 1]


def complete_groups(chunks):
    levels = sum(chunks)
    ends = [sum(chunks[: t + 1]) for t in range(len(chunks))]
    return [0] + [-(-FIELDS * e // 4) if e == levels else FIELDS * e // 4 for e in ends]


def analysis_kernel(
    wide_count, narrow_count, levels, chunks,
    traj_ref, depart_ref, back_ref, weight_ref, wave_ref, out_ref,
    depart, back, weight, wave, pool, spread, response, sums, sent, landed, fields, result,
    outgoing, returned, tall, up_out, down_out, up_in, down_in,
    load_sem, local_sem, send_sem, recv_sem, halo_send, halo_recv, back_send, back_recv,
):
    me = lax.axis_index("wide")
    band = lax.axis_index("narrow")
    has_above = band > 0
    has_below = band < narrow_count - 1
    total_levels = traj_ref.shape[1]
    fine_rows, fine_cols = traj_ref.shape[2:]
    halves = fine_rows // (SUB * COARSEN)
    rows = halves * SUB
    cycle = wave.shape[1]
    half = cycle // 2
    cols = cycle // wide_count
    padded = fields.shape[1]
    line = PACKED * SUB
    owners = -(-total_levels // levels)
    turns = len(chunks)
    starts = [sum(chunks[:t]) for t in range(turns)]
    ends = [starts[t] + chunks[t] for t in range(turns)]
    group_bounds = complete_groups(chunks)

    barrier = pltpu.get_barrier_semaphore()
    for k in range(1, wide_count):
        pl.semaphore_signal(
            barrier, inc=1, device_id=(lax.rem(me + k, wide_count), band), device_id_type=MESH
        )

    @pl.when(has_above)
    def _():
        pl.semaphore_signal(barrier, inc=1, device_id=(me, band - 1), device_id_type=MESH)

    @pl.when(has_below)
    def _():
        pl.semaphore_signal(barrier, inc=1, device_id=(me, band + 1), device_id_type=MESH)

    runs = [(0, rows - HALO), (SUB, HALO)]

    def loads(h):
        copies = []
        for q, first in enumerate(runs[h]):
            part = pl.ds(first, HALO)
            fine = pl.ds(first * COARSEN, HALO * COARSEN)
            moves = [
                (back_ref.at[:, part], back.at[:, part]),
                (depart_ref.at[:, part], depart.at[:, part]),
                (weight_ref.at[part], weight.at[part]),
                (traj_ref.at[0, :, fine], out_ref.at[0, :, fine]),
            ]
            copies.append(
                [pltpu.make_async_copy(src, dst, load_sem.at[h, q, n]) for n, (src, dst) in enumerate(moves)]
            )
        return copies

    loading = [loads(h) for h in range(halves)]
    for h in range(halves):
        for n in range(4):
            for q in range(2):
                loading[h][q][n].start()
    load_wave = pltpu.make_async_copy(wave_ref, wave, local_sem.at[0])
    load_wave.start()
    load_rest = pltpu.make_async_copy(
        traj_ref.at[pl.ds(1, FIELDS - 1)], out_ref.at[pl.ds(1, FIELDS - 1)], local_sem.at[1]
    )

    lane = lax.broadcasted_iota(jnp.int32, (fine_cols, LANES), 1)
    source = lax.broadcasted_iota(jnp.int32, (fine_cols, LANES), 0)
    pool[...] = (lane == FIELDS % 4 * cols + source // COARSEN).astype(jnp.float32).astype(jnp.bfloat16)

    def item(index, row):
        if index < FIELDS:
            return back[index, row]
        if index < FIELDS + 2:
            return weight[row]
        return depart[index - FIELDS - 2, row]

    def pack(h):
        for n in range(3):
            for q in range(2):
                loading[h][q][n].wait()
        for group in range(PACKED):
            for r in range(SUB):
                stacked = jnp.concatenate([item(4 * group + j, runs[h][r // HALO] + r % HALO) for j in range(4)], axis=0)
                sent[h, pl.ds(group * SUB + r, total_levels, stride=line), :] = stacked.T
        for q in range(2):
            loading[h][q][3].wait()
        fine = jnp.concatenate(
            [out_ref[0, :, first * COARSEN : (first + HALO) * COARSEN] for first in runs[h]], axis=1
        )
        count = total_levels * SUB
        sums[...] = dot(fine.reshape(count * COARSEN, fine_cols), pool[...])
        total = sums[pl.ds(0, count, stride=COARSEN), :]
        for t in range(1, COARSEN):
            total = total + sums[pl.ds(t, count, stride=COARSEN), :]
        drift = advection_scale * jnp.tanh(total * (1.0 / (COARSEN * COARSEN)))
        is_drift = lax.broadcasted_iota(jnp.int32, (SUB, LANES), 1) // cols == FIELDS % 4
        for level in range(total_levels):
            at = level * line + FIELDS // 4 * SUB
            sent[h, at : at + SUB] = jnp.where(
                is_drift, drift[level * SUB : (level + 1) * SUB], sent[h, at : at + SUB]
            )

    split = max(2, turns - 2)
    pairs = [(0, min(2, turns))] + [(t, t + 1) for t in range(2, split)]
    if split < turns:
        pairs.append((split, turns))
    pieces = []
    for n, (first, end) in enumerate(pairs):
        pieces += [(first, end, 0), (n, n + 1, 1)]
    pieces += [(t, t + 1, 1) for t in range(len(pairs), turns)]

    def piece_copies(n):
        first, end, h = pieces[n]
        begin = starts[first] * line
        size = ends[end - 1] * line - begin
        copies = []
        for k in range(1, wide_count):
            peer = lax.rem(me + k, wide_count)
            copies.append(
                pltpu.make_async_remote_copy(
                    src_ref=sent.at[h, pl.ds(peer * (levels * line) + begin, size)],
                    dst_ref=landed.at[me, h, pl.ds(begin, size)],
                    send_sem=send_sem.at[n, k],
                    recv_sem=recv_sem.at[n, k],
                    device_id=(peer, band),
                    device_id_type=MESH,
                )
            )
        return copies

    sends = [piece_copies(n) for n in range(len(pieces))]
    pack(0)
    neighbours = has_above.astype(jnp.int32) + has_below.astype(jnp.int32)
    pl.semaphore_wait(barrier, wide_count - 1 + neighbours)
    for copy in sends[0]:
        copy.start()
    pack(1)
    for copies in sends[1:]:
        for copy in copies:
            copy.start()
    keeps = [
        pltpu.make_async_copy(
            sent.at[h, pl.ds(me * (levels * line), levels * line)], landed.at[me, h], local_sem.at[2 + h]
        )
        for h in range(halves)
    ]
    for copy in keeps:
        copy.start()
    load_rest.start()

    place = lax.broadcasted_iota(jnp.int32, (padded, cycle), 0)
    row_index = jnp.where(place < rows + HALO, place, place - padded) + band * rows
    wavenumber = lax.broadcasted_iota(jnp.int32, (padded, cycle), 1)
    folded = jnp.minimum(wavenumber, cycle - wavenumber).astype(jnp.float32)
    total_rows = rows * narrow_count
    latitude = jnp.pi * ((row_index.astype(jnp.float32) + 0.5) / total_rows - 0.5)
    inside = (row_index >= 0) & (row_index < total_rows)
    cutoff = jnp.where(inside, 0.5 * cycle * jnp.cos(latitude), 1.0)
    squared = (folded / cutoff) * (folded / cutoff)
    response[...] = jnp.where(inside, 1.0 / (1.0 + squared * squared), 0.0) / cycle

    source = lax.broadcasted_iota(jnp.int32, spread.shape, 0) % LANES
    lane = lax.broadcasted_iota(jnp.int32, spread.shape, 1)
    spread[...] = (
        (source == lane // LANES * cols + lane % LANES // COARSEN).astype(jnp.float32).astype(jnp.bfloat16)
    )

    @pl.when(jnp.logical_not(has_below))
    def _():
        up_in[...] = jnp.zeros_like(up_in)

    @pl.when(jnp.logical_not(has_above))
    def _():
        down_in[...] = jnp.zeros_like(down_in)

    for copy in keeps:
        copy.wait()

    low_lines = lax.broadcasted_iota(jnp.int32, (SUB, half), 0) < HALO
    low_half = low_lines[:, :LANES]

    tiles = cycle // LANES

    def landed_items(level, h):
        for group in range(PACKED):
            at = pl.ds(level * line + group * SUB, SUB)
            by_tile = [
                block_transpose([landed[4 * tile + m, h, at] for m in range(4)], cols) for tile in range(tiles)
            ]
            for j in range(4):
                at = level * ITEMS + 4 * group + j
                values = [by_tile[tile][j] for tile in range(tiles)]
                for q, first in enumerate(runs[h]):
                    for tile in range(tiles):
                        fields[at, first : first + HALO, tile * LANES : (tile + 1) * LANES] = values[tile][
                            q * HALO : (q + 1) * HALO
                        ]
                yield at, values

    def unpack_edges(level):
        for at, values in landed_items(level, 0):
            for tile in range(tiles // 2):
                a, b = values[tile], values[tile + tiles // 2]
                lanes = slice(tile * LANES, (tile + 1) * LANES)
                up_out[at, :, lanes] = jnp.where(low_half, a, pltpu.roll(b, HALO, 0))
                down_out[at, :, lanes] = jnp.where(low_half, pltpu.roll(a, HALO, 0), b)

    def unpack_middle(level):
        for _ in landed_items(level, 1):
            pass

    def halo_copies(first, end):
        part = pl.ds(starts[first] * ITEMS, (ends[end - 1] - starts[first]) * ITEMS)
        up_copy = pltpu.make_async_remote_copy(
            src_ref=up_out.at[part], dst_ref=up_in.at[part],
            send_sem=halo_send.at[first, 0], recv_sem=halo_recv.at[first, 0],
            device_id=(me, band - 1), device_id_type=MESH,
        )
        down_copy = pltpu.make_async_remote_copy(
            src_ref=down_out.at[part], dst_ref=down_in.at[part],
            send_sem=halo_send.at[first, 1], recv_sem=halo_recv.at[first, 1],
            device_id=(me, band + 1), device_id_type=MESH,
        )
        return up_copy, down_copy

    def take_halo(level):
        for index in range(ITEMS):
            at = level * ITEMS + index
            below, above = up_in[at], down_in[at]
            fields[at, rows:padded, 0:half] = jnp.where(low_lines, below, pltpu.roll(above, HALO, 0))
            fields[at, rows:padded, half:cycle] = jnp.where(low_lines, pltpu.roll(below, HALO, 0), above)

    def transform(q):
        count = q.shape[0]
        high, low = split_bf16(q)
        wave_high, wave_low = wave[0:cycle], wave[cycle : 2 * cycle]
        both = dot(jnp.concatenate([high, low], axis=0), wave_high)
        return both[:count] + both[count:] + dot(high, wave_low)

    def zonal(q):
        shape = q.shape
        spectrum = transform(q.reshape(-1, cycle)).reshape(shape) * response[...]
        return transform(spectrum.reshape(-1, cycle)).reshape(shape)

    def sweep(turn):
        at, chunk = starts[turn], chunks[turn]
        block = fields[at * ITEMS : (at + chunk) * ITEMS].reshape(chunk, ITEMS, padded, cycle)
        background = block[:, :FIELDS]
        drift = block[:, FIELDS : FIELDS + 1]
        observed = block[:, FIELDS + 1 : FIELDS + 2]
        departure = block[:, FIELDS + 2 :]
        state = background
        for _ in range(STEPS):
            state = zonal(stencil(state, drift))
        costate = observed * (state - departure)
        for _ in range(STEPS):
            costate = stencil_transposed(zonal(costate), drift)
        increment = background - descent_step * ((background - background) + costate)
        result[at * FIELDS : (at + chunk) * FIELDS] = increment.reshape(chunk * FIELDS, padded, cycle)[:, :rows]

    def repack(group):
        for tile in range(cycle // LANES):
            parts = [result[4 * group + j, :, tile * LANES : (tile + 1) * LANES] for j in range(4)]
            for m, value in enumerate(block_transpose(parts, cols)):
                outgoing[4 * tile + m, group] = value

    backs = {}

    def receive(n):
        first, end, h = pieces[n]
        for copy in sends[n]:
            copy.wait_recv()
        for level in range(starts[first], ends[end - 1]):
            if h == 0:
                unpack_edges(level)
            else:
                unpack_middle(level)
        if h == 0:
            up_copy, down_copy = halo_copies(first, end)
            pl.when(has_above)(up_copy.start)
            pl.when(has_below)(down_copy.start)

    def await_halo(first, end):
        up_copy, down_copy = halo_copies(first, end)
        pl.when(has_below)(up_copy.wait_recv)
        pl.when(has_above)(down_copy.wait_recv)

    def compute(turn):
        for first, end in pairs:
            if first == turn:
                await_halo(first, end)

        for level in range(starts[turn], ends[turn]):
            take_halo(level)
        sweep(turn)
        first, end = group_bounds[turn : turn + 2]
        for group in range(first, end):
            repack(group)
        part = pl.ds(first, end - first)
        keep_back = pltpu.make_async_copy(
            outgoing.at[me, part], returned.at[me, part], back_send.at[turn, 0]
        )
        keep_back.start()
        backs[turn, 0] = keep_back
        for k in range(1, wide_count):
            peer = lax.rem(me + k, wide_count)
            copy = pltpu.make_async_remote_copy(
                src_ref=outgoing.at[peer, part],
                dst_ref=returned.at[me, part],
                send_sem=back_send.at[turn, k],
                recv_sem=back_recv.at[turn, k],
                device_id=(peer, band),
                device_id_type=MESH,
            )
            copy.start()
            backs[turn, k] = copy

    def finish(turn):
        first, end = group_bounds[turn : turn + 2]
        count = end - first
        span = count * rows
        backs[turn, 0].wait()
        for k in range(1, wide_count):
            backs[turn, k].wait_recv()

        def owner(s):
            part = returned[s, first:end].reshape(span, LANES)
            for t in range(COARSEN):
                tall[s, pl.ds(t, span, stride=COARSEN), :] = part
            operand = jnp.concatenate(split_bf16(tall[s, 0 : span * COARSEN]), axis=1)
            wide = dot(operand, spread[...])

            def put(group, j, place):
                f = place % FIELDS
                level = s * levels + place // FIELDS
                fine = wide[group * fine_rows : (group + 1) * fine_rows, j * LANES : j * LANES + fine_cols]
                out_ref[f, level] = (out_ref[f, level].astype(jnp.float32) + fine).astype(jnp.bfloat16)

            for group in range(count):
                for j in range(4):
                    place = 4 * (first + group) + j
                    if place < levels * FIELDS and s * levels + place // FIELDS < total_levels:
                        put(group, j, place)

        for s in range(owners):
            owner(s)

    load_wave.wait()
    waiting = []
    for n, (first, _, h) in enumerate(pieces):
        receive(n)
        if h == 1:
            waiting.append(first)
        if h == 0 or all(part == 1 for _, _, part in pieces[n:]):
            for turn in waiting:
                compute(turn)
            waiting = []
    load_rest.wait()
    for turn in range(turns):
        finish(turn)

    for copies in sends:
        for copy in copies:
            copy.wait_send()
    for first, end in pairs:
        up_copy, down_copy = halo_copies(first, end)
        pl.when(has_above)(up_copy.wait_send)
        pl.when(has_below)(down_copy.wait_send)
    for turn in range(turns):
        for k in range(1, wide_count):
            backs[turn, k].wait_send()


def shards(trajectory, innovation, background, obs_weight):
    wide_count = lax.axis_size("wide")
    narrow_count = lax.axis_size("narrow")
    fields, total_levels, rows, cols = innovation.shape
    fine_rows, fine_cols = trajectory.shape[2:]
    cycle = cols * wide_count
    levels = -(-total_levels // wide_count)
    chunks = chunk_sizes(levels)
    turns = len(chunks)
    bounds = complete_groups(chunks)
    groups = bounds[-1]
    largest = max(end - first for first, end in zip(bounds, bounds[1:]))
    padded = rows + 2 * HALO
    halves = rows // SUB
    line = PACKED * SUB

    phase = np.arange(cycle)[:, None] * np.arange(cycle)[None, :] % cycle
    wave = np.cos(2.0 * np.pi / cycle * phase) + np.sin(2.0 * np.pi / cycle * phase)
    wave = wave.astype(np.float32)
    wave_high = wave.astype(jnp.bfloat16)
    wave_low = (wave - wave_high.astype(np.float32)).astype(jnp.bfloat16)
    wave = jnp.asarray(np.concatenate([wave_high, wave_low]))

    hbm = pl.BlockSpec(memory_space=pltpu.HBM)
    vmem = pl.BlockSpec(memory_space=pltpu.VMEM)
    f32 = jnp.float32
    bf16 = jnp.bfloat16
    dma = pltpu.SemaphoreType.DMA
    return pl.pallas_call(
        functools.partial(analysis_kernel, wide_count, narrow_count, levels, chunks),
        in_specs=[hbm] * 5,
        out_specs=vmem,
        out_shape=pltpu.VMEM(trajectory.shape, bf16),
        scratch_shapes=[
            pltpu.VMEM((fields, rows, cols, total_levels), f32),
            pltpu.VMEM((fields, rows, cols, total_levels), f32),
            pltpu.VMEM((rows, cols, total_levels), f32),
            pltpu.VMEM((2 * cycle, cycle), bf16),
            pltpu.VMEM((fine_cols, LANES), bf16),
            pltpu.VMEM((2 * LANES, 4 * LANES), bf16),
            pltpu.VMEM((padded, cycle), f32),
            pltpu.VMEM((total_levels * SUB * COARSEN, LANES), f32),
            pltpu.VMEM((halves, wide_count * levels * line, LANES), f32),
            pltpu.VMEM((wide_count, halves, levels * line, LANES), f32),
            pltpu.VMEM((levels * ITEMS, padded, cycle), f32),
            pltpu.VMEM((groups * 4, rows, cycle), f32),
            pltpu.VMEM((wide_count, groups, rows, LANES), f32),
            pltpu.VMEM((wide_count, groups, rows, LANES), f32),
            pltpu.VMEM((wide_count, largest * fine_rows, LANES), f32),
            pltpu.VMEM((levels * ITEMS, SUB, cycle // 2), f32),
            pltpu.VMEM((levels * ITEMS, SUB, cycle // 2), f32),
            pltpu.VMEM((levels * ITEMS, SUB, cycle // 2), f32),
            pltpu.VMEM((levels * ITEMS, SUB, cycle // 2), f32),
            dma((halves, 2, 4)),
            dma((2 + halves,)),
            dma((2 * turns, wide_count)),
            dma((2 * turns, wide_count)),
            dma((turns, 2)),
            dma((turns, 2)),
            dma((turns, wide_count)),
            dma((turns, wide_count)),
        ],
        compiler_params=pltpu.CompilerParams(
            collective_id=0, has_side_effects=True, vmem_limit_bytes=40 * 1024 * 1024
        ),
        name="analysis",
    )(
        *(
            pltpu.with_memory_space_constraint(x, pltpu.HBM)
            for x in (
                trajectory,
                innovation.transpose(0, 2, 3, 1),
                background.transpose(0, 2, 3, 1),
                obs_weight.transpose(1, 2, 0),
                wave,
            )
        )
    )


def solution(mesh):
    in_specs = (
        P(None, None, "narrow", "wide"),
        P(None, None, "narrow", "wide"),
        P(None, None, "narrow", "wide"),
        P(None, "narrow", "wide"),
    )
    out_specs = P(None, None, "narrow", "wide")
    return jax.shard_map(shards, mesh=mesh, in_specs=in_specs, out_specs=out_specs, check_vma=False)
```

```python
import functools

import jax
import jax.numpy as jnp
import numpy as np
from jax import lax
from jax.experimental import pallas as pl
from jax.experimental.pallas import tpu as pltpu
from jax.sharding import PartitionSpec as P

MESH = pl.DeviceIdType.MESH
FIELDS = 5
COARSEN = 4
STEPS = 2
LANES = 128
SUB = 8
HALO = 2 * STEPS
ITEMS = 2 * FIELDS + 2
PACKED = ITEMS // 4

diffusion = 0.2
advection_scale = 0.3
descent_step = 1.0


def split_bf16(x):
    high = x.astype(jnp.bfloat16)
    low = (x - high.astype(jnp.float32)).astype(jnp.bfloat16)
    return high, low


def dot(a, b):
    return jnp.dot(a, b, preferred_element_type=jnp.float32)


def block_transpose(tiles, block):
    lane = lax.broadcasted_iota(jnp.int32, tiles[0].shape, len(tiles[0].shape) - 1) // block
    axis = len(tiles[0].shape) - 1
    tiles = list(tiles)
    for step in (2, 1):
        upper = (lane // step) % 2 == 1
        for first in range(4):
            if (first // step) % 2 == 0:
                second = first + step
                a, b = tiles[first], tiles[second]
                tiles[first] = jnp.where(upper, pltpu.roll(b, step * block, axis), a)
                tiles[second] = jnp.where(upper, b, pltpu.roll(a, LANES - step * block, axis))
    return tiles


def stencil(q, drift):
    rows, cycle = q.shape[-2:]
    north = pltpu.roll(q, 1, q.ndim - 2)
    south = pltpu.roll(q, rows - 1, q.ndim - 2)
    east = pltpu.roll(q, cycle - 1, q.ndim - 1)
    west = pltpu.roll(q, 1, q.ndim - 1)
    return (
        (1.0 - 4.0 * diffusion) * q
        + diffusion * (north + south)
        + (diffusion + drift) * east
        + (diffusion - drift) * west
    )


def stencil_transposed(g, drift):
    rows, cycle = g.shape[-2:]
    north = pltpu.roll(g, 1, g.ndim - 2)
    south = pltpu.roll(g, rows - 1, g.ndim - 2)
    return (
        (1.0 - 4.0 * diffusion) * g
        + diffusion * (north + south)
        + pltpu.roll((diffusion + drift) * g, 1, g.ndim - 1)
        + pltpu.roll((diffusion - drift) * g, cycle - 1, g.ndim - 1)
    )


def chunk_sizes(levels):
    if levels < 6:
        return [1] + [2] * ((levels - 1) // 2) + [1] * ((levels - 1) % 2)
    middle = levels - 6
    return [1, 2] + [3] * (middle // 3) + [middle % 3] * (middle % 3 > 0) + [2, 1]


def complete_groups(chunks):
    levels = sum(chunks)
    ends = [sum(chunks[: t + 1]) for t in range(len(chunks))]
    return [0] + [-(-FIELDS * e // 4) if e == levels else FIELDS * e // 4 for e in ends]


def analysis_kernel(
    wide_count, narrow_count, levels, chunks,
    traj_ref, depart_ref, back_ref, weight_ref, wave_ref, out_ref,
    depart, back, weight, wave, pool, spread, response, sums, sent, landed, fields, result,
    outgoing, returned, tall, up_out, down_out, up_in, down_in,
    load_sem, local_sem, send_sem, recv_sem, halo_send, halo_recv, back_send, back_recv,
):
    me = lax.axis_index("wide")
    band = lax.axis_index("narrow")
    has_above = band > 0
    has_below = band < narrow_count - 1
    total_levels = traj_ref.shape[1]
    fine_rows, fine_cols = traj_ref.shape[2:]
    halves = fine_rows // (SUB * COARSEN)
    rows = halves * SUB
    cycle = wave.shape[1]
    half = cycle // 2
    cols = cycle // wide_count
    padded = fields.shape[1]
    line = PACKED * SUB
    owners = -(-total_levels // levels)
    turns = len(chunks)
    starts = [sum(chunks[:t]) for t in range(turns)]
    ends = [starts[t] + chunks[t] for t in range(turns)]
    group_bounds = complete_groups(chunks)

    barrier = pltpu.get_barrier_semaphore()
    for k in range(1, wide_count):
        pl.semaphore_signal(
            barrier, inc=1, device_id=(lax.rem(me + k, wide_count), band), device_id_type=MESH
        )

    @pl.when(has_above)
    def _():
        pl.semaphore_signal(barrier, inc=1, device_id=(me, band - 1), device_id_type=MESH)

    @pl.when(has_below)
    def _():
        pl.semaphore_signal(barrier, inc=1, device_id=(me, band + 1), device_id_type=MESH)

    runs = [(0, rows - HALO), (SUB, HALO)]

    def loads(h):
        copies = []
        for q, first in enumerate(runs[h]):
            part = pl.ds(first, HALO)
            fine = pl.ds(first * COARSEN, HALO * COARSEN)
            moves = [
                (back_ref.at[:, part], back.at[:, part]),
                (depart_ref.at[:, part], depart.at[:, part]),
                (weight_ref.at[part], weight.at[part]),
                (traj_ref.at[0, :, fine], out_ref.at[0, :, fine]),
            ]
            copies.append(
                [pltpu.make_async_copy(src, dst, load_sem.at[h, q, n]) for n, (src, dst) in enumerate(moves)]
            )
        return copies

    loading = [loads(h) for h in range(halves)]
    for h in range(halves):
        for n in range(4):
            for q in range(2):
                loading[h][q][n].start()
    load_wave = pltpu.make_async_copy(wave_ref, wave, local_sem.at[0])
    load_wave.start()
    load_rest = pltpu.make_async_copy(
        traj_ref.at[pl.ds(1, FIELDS - 1)], out_ref.at[pl.ds(1, FIELDS - 1)], local_sem.at[1]
    )

    lane = lax.broadcasted_iota(jnp.int32, (fine_cols, LANES), 1)
    source = lax.broadcasted_iota(jnp.int32, (fine_cols, LANES), 0)
    pool[...] = (lane == FIELDS % 4 * cols + source // COARSEN).astype(jnp.float32).astype(jnp.bfloat16)

    def item(index, row):
        if index < FIELDS:
            return back[index, row]
        if index < FIELDS + 2:
            return weight[row]
        return depart[index - FIELDS - 2, row]

    def pack(h):
        for n in range(3):
            for q in range(2):
                loading[h][q][n].wait()
        for group in range(PACKED):
            for r in range(SUB):
                stacked = jnp.concatenate([item(4 * group + j, runs[h][r // HALO] + r % HALO) for j in range(4)], axis=0)
                sent[h, pl.ds(group * SUB + r, total_levels, stride=line), :] = stacked.T
        for q in range(2):
            loading[h][q][3].wait()
        fine = jnp.concatenate(
            [out_ref[0, :, first * COARSEN : (first + HALO) * COARSEN] for first in runs[h]], axis=1
        )
        count = total_levels * SUB
        sums[...] = dot(fine.reshape(count * COARSEN, fine_cols), pool[...])
        total = sums[pl.ds(0, count, stride=COARSEN), :]
        for t in range(1, COARSEN):
            total = total + sums[pl.ds(t, count, stride=COARSEN), :]
        drift = advection_scale * jnp.tanh(total * (1.0 / (COARSEN * COARSEN)))
        is_drift = lax.broadcasted_iota(jnp.int32, (SUB, LANES), 1) // cols == FIELDS % 4
        for level in range(total_levels):
            at = level * line + FIELDS // 4 * SUB
            sent[h, at : at + SUB] = jnp.where(
                is_drift, drift[level * SUB : (level + 1) * SUB], sent[h, at : at + SUB]
            )

    split = max(2, turns - 2)
    pairs = [(0, min(2, turns))] + [(t, t + 1) for t in range(2, split)]
    if split < turns:
        pairs.append((split, turns))
    pieces = []
    for n, (first, end) in enumerate(pairs):
        pieces += [(first, end, 0), (n, n + 1, 1)]
    pieces += [(t, t + 1, 1) for t in range(len(pairs), turns)]

    def piece_copies(n):
        first, end, h = pieces[n]
        begin = starts[first] * line
        size = ends[end - 1] * line - begin
        copies = []
        for k in range(1, wide_count):
            peer = lax.rem(me + k, wide_count)
            copies.append(
                pltpu.make_async_remote_copy(
                    src_ref=sent.at[h, pl.ds(peer * (levels * line) + begin, size)],
                    dst_ref=landed.at[me, h, pl.ds(begin, size)],
                    send_sem=send_sem.at[n, k],
                    recv_sem=recv_sem.at[n, k],
                    device_id=(peer, band),
                    device_id_type=MESH,
                )
            )
        return copies

    sends = [piece_copies(n) for n in range(len(pieces))]
    pack(0)
    neighbours = has_above.astype(jnp.int32) + has_below.astype(jnp.int32)
    pl.semaphore_wait(barrier, wide_count - 1 + neighbours)
    for copy in sends[0]:
        copy.start()
    pack(1)
    for copies in sends[1:]:
        for copy in copies:
            copy.start()
    keeps = [
        pltpu.make_async_copy(
            sent.at[h, pl.ds(me * (levels * line), levels * line)], landed.at[me, h], local_sem.at[2 + h]
        )
        for h in range(halves)
    ]
    for copy in keeps:
        copy.start()
    load_rest.start()

    place = lax.broadcasted_iota(jnp.int32, (padded, cycle), 0)
    row_index = jnp.where(place < rows + HALO, place, place - padded) + band * rows
    wavenumber = lax.broadcasted_iota(jnp.int32, (padded, cycle), 1)
    folded = jnp.minimum(wavenumber, cycle - wavenumber).astype(jnp.float32)
    total_rows = rows * narrow_count
    latitude = jnp.pi * ((row_index.astype(jnp.float32) + 0.5) / total_rows - 0.5)
    inside = (row_index >= 0) & (row_index < total_rows)
    cutoff = jnp.where(inside, 0.5 * cycle * jnp.cos(latitude), 1.0)
    squared = (folded / cutoff) * (folded / cutoff)
    response[...] = jnp.where(inside, 1.0 / (1.0 + squared * squared), 0.0) / cycle

    source = lax.broadcasted_iota(jnp.int32, spread.shape, 0) % LANES
    lane = lax.broadcasted_iota(jnp.int32, spread.shape, 1)
    spread[...] = (
        (source == lane // LANES * cols + lane % LANES // COARSEN).astype(jnp.float32).astype(jnp.bfloat16)
    )

    @pl.when(jnp.logical_not(has_below))
    def _():
        up_in[...] = jnp.zeros_like(up_in)

    @pl.when(jnp.logical_not(has_above))
    def _():
        down_in[...] = jnp.zeros_like(down_in)

    for copy in keeps:
        copy.wait()

    low_lines = lax.broadcasted_iota(jnp.int32, (SUB, half), 0) < HALO
    low_half = low_lines[:, :LANES]

    tiles = cycle // LANES

    def landed_items(level, h):
        for group in range(PACKED):
            at = pl.ds(level * line + group * SUB, SUB)
            by_tile = [
                block_transpose([landed[4 * tile + m, h, at] for m in range(4)], cols) for tile in range(tiles)
            ]
            for j in range(4):
                at = level * ITEMS + 4 * group + j
                values = [by_tile[tile][j] for tile in range(tiles)]
                for q, first in enumerate(runs[h]):
                    for tile in range(tiles):
                        fields[at, first : first + HALO, tile * LANES : (tile + 1) * LANES] = values[tile][
                            q * HALO : (q + 1) * HALO
                        ]
                yield at, values

    def unpack_edges(level):
        for at, values in landed_items(level, 0):
            for tile in range(tiles // 2):
                a, b = values[tile], values[tile + tiles // 2]
                lanes = slice(tile * LANES, (tile + 1) * LANES)
                up_out[at, :, lanes] = jnp.where(low_half, a, pltpu.roll(b, HALO, 0))
                down_out[at, :, lanes] = jnp.where(low_half, pltpu.roll(a, HALO, 0), b)

    def unpack_middle(level):
        for _ in landed_items(level, 1):
            pass

    def halo_copies(first, end):
        part = pl.ds(starts[first] * ITEMS, (ends[end - 1] - starts[first]) * ITEMS)
        up_copy = pltpu.make_async_remote_copy(
            src_ref=up_out.at[part], dst_ref=up_in.at[part],
            send_sem=halo_send.at[first, 0], recv_sem=halo_recv.at[first, 0],
            device_id=(me, band - 1), device_id_type=MESH,
        )
        down_copy = pltpu.make_async_remote_copy(
            src_ref=down_out.at[part], dst_ref=down_in.at[part],
            send_sem=halo_send.at[first, 1], recv_sem=halo_recv.at[first, 1],
            device_id=(me, band + 1), device_id_type=MESH,
        )
        return up_copy, down_copy

    def take_halo(level):
        for index in range(ITEMS):
            at = level * ITEMS + index
            below, above = up_in[at], down_in[at]
            fields[at, rows:padded, 0:half] = jnp.where(low_lines, below, pltpu.roll(above, HALO, 0))
            fields[at, rows:padded, half:cycle] = jnp.where(low_lines, pltpu.roll(below, HALO, 0), above)

    def transform(q):
        count = q.shape[0]
        high, low = split_bf16(q)
        wave_high, wave_low = wave[0:cycle], wave[cycle : 2 * cycle]
        both = dot(jnp.concatenate([high, low], axis=0), wave_high)
        return both[:count] + both[count:] + dot(high, wave_low)

    def zonal(q):
        shape = q.shape
        spectrum = transform(q.reshape(-1, cycle)).reshape(shape) * response[...]
        return transform(spectrum.reshape(-1, cycle)).reshape(shape)

    def sweep(turn):
        at, chunk = starts[turn], chunks[turn]
        block = fields[at * ITEMS : (at + chunk) * ITEMS].reshape(chunk, ITEMS, padded, cycle)
        background = block[:, :FIELDS]
        drift = block[:, FIELDS : FIELDS + 1]
        observed = block[:, FIELDS + 1 : FIELDS + 2]
        departure = block[:, FIELDS + 2 :]
        state = background
        for _ in range(STEPS):
            state = zonal(stencil(state, drift))
        costate = observed * (state - departure)
        for _ in range(STEPS):
            costate = stencil_transposed(zonal(costate), drift)
        increment = background - descent_step * ((background - background) + costate)
        result[at * FIELDS : (at + chunk) * FIELDS] = increment.reshape(chunk * FIELDS, padded, cycle)[:, :rows]

    def repack(group):
        for tile in range(cycle // LANES):
            parts = [result[4 * group + j, :, tile * LANES : (tile + 1) * LANES] for j in range(4)]
            for m, value in enumerate(block_transpose(parts, cols)):
                outgoing[4 * tile + m, group] = value

    backs = {}

    def receive(n):
        first, end, h = pieces[n]
        for copy in sends[n]:
            copy.wait_recv()
        for level in range(starts[first], ends[end - 1]):
            if h == 0:
                unpack_edges(level)
            else:
                unpack_middle(level)
        if h == 0:
            up_copy, down_copy = halo_copies(first, end)
            pl.when(has_above)(up_copy.start)
            pl.when(has_below)(down_copy.start)

    def await_halo(first, end):
        up_copy, down_copy = halo_copies(first, end)
        pl.when(has_below)(up_copy.wait_recv)
        pl.when(has_above)(down_copy.wait_recv)

    def compute(turn):
        for first, end in pairs:
            if first == turn:
                await_halo(first, end)

        for level in range(starts[turn], ends[turn]):
            take_halo(level)
        sweep(turn)
        first, end = group_bounds[turn : turn + 2]
        for group in range(first, end):
            repack(group)
        part = pl.ds(first, end - first)
        keep_back = pltpu.make_async_copy(
            outgoing.at[me, part], returned.at[me, part], back_send.at[turn, 0]
        )
        keep_back.start()
        backs[turn, 0] = keep_back
        for k in range(1, wide_count):
            peer = lax.rem(me + k, wide_count)
            copy = pltpu.make_async_remote_copy(
                src_ref=outgoing.at[peer, part],
                dst_ref=returned.at[me, part],
                send_sem=back_send.at[turn, k],
                recv_sem=back_recv.at[turn, k],
                device_id=(peer, band),
                device_id_type=MESH,
            )
            copy.start()
            backs[turn, k] = copy

    def finish(turn):
        first, end = group_bounds[turn : turn + 2]
        count = end - first
        span = count * rows
        backs[turn, 0].wait()
        for k in range(1, wide_count):
            backs[turn, k].wait_recv()

        def owner(s):
            part = returned[s, first:end].reshape(span, LANES)
            for t in range(COARSEN):
                tall[s, pl.ds(t, span, stride=COARSEN), :] = part
            operand = jnp.concatenate(split_bf16(tall[s, 0 : span * COARSEN]), axis=1)
            wide = dot(operand, spread[...])

            def put(group, j, place):
                f = place % FIELDS
                level = s * levels + place // FIELDS
                fine = wide[group * fine_rows : (group + 1) * fine_rows, j * LANES : j * LANES + fine_cols]
                out_ref[f, level] = (out_ref[f, level].astype(jnp.float32) + fine).astype(jnp.bfloat16)

            for group in range(count):
                for j in range(4):
                    place = 4 * (first + group) + j
                    if place < levels * FIELDS and s * levels + place // FIELDS < total_levels:
                        put(group, j, place)

        for s in range(owners):
            owner(s)

    load_wave.wait()
    waiting = []
    for n, (first, _, h) in enumerate(pieces):
        receive(n)
        if h == 1:
            waiting.append(first)
        if h == 0 or first > 0 or len(pairs) == 1:
            for turn in waiting:
                compute(turn)
            waiting = []
    load_rest.wait()
    for turn in range(turns):
        finish(turn)

    for copies in sends:
        for copy in copies:
            copy.wait_send()
    for first, end in pairs:
        up_copy, down_copy = halo_copies(first, end)
        pl.when(has_above)(up_copy.wait_send)
        pl.when(has_below)(down_copy.wait_send)
    for turn in range(turns):
        for k in range(1, wide_count):
            backs[turn, k].wait_send()


def shards(trajectory, innovation, background, obs_weight):
    wide_count = lax.axis_size("wide")
    narrow_count = lax.axis_size("narrow")
    fields, total_levels, rows, cols = innovation.shape
    fine_rows, fine_cols = trajectory.shape[2:]
    cycle = cols * wide_count
    levels = -(-total_levels // wide_count)
    chunks = chunk_sizes(levels)
    turns = len(chunks)
    bounds = complete_groups(chunks)
    groups = bounds[-1]
    largest = max(end - first for first, end in zip(bounds, bounds[1:]))
    padded = rows + 2 * HALO
    halves = rows // SUB
    line = PACKED * SUB

    phase = np.arange(cycle)[:, None] * np.arange(cycle)[None, :] % cycle
    wave = np.cos(2.0 * np.pi / cycle * phase) + np.sin(2.0 * np.pi / cycle * phase)
    wave = wave.astype(np.float32)
    wave_high = wave.astype(jnp.bfloat16)
    wave_low = (wave - wave_high.astype(np.float32)).astype(jnp.bfloat16)
    wave = jnp.asarray(np.concatenate([wave_high, wave_low]))

    hbm = pl.BlockSpec(memory_space=pltpu.HBM)
    vmem = pl.BlockSpec(memory_space=pltpu.VMEM)
    f32 = jnp.float32
    bf16 = jnp.bfloat16
    dma = pltpu.SemaphoreType.DMA
    return pl.pallas_call(
        functools.partial(analysis_kernel, wide_count, narrow_count, levels, chunks),
        in_specs=[hbm] * 5,
        out_specs=vmem,
        out_shape=pltpu.VMEM(trajectory.shape, bf16),
        scratch_shapes=[
            pltpu.VMEM((fields, rows, cols, total_levels), f32),
            pltpu.VMEM((fields, rows, cols, total_levels), f32),
            pltpu.VMEM((rows, cols, total_levels), f32),
            pltpu.VMEM((2 * cycle, cycle), bf16),
            pltpu.VMEM((fine_cols, LANES), bf16),
            pltpu.VMEM((2 * LANES, 4 * LANES), bf16),
            pltpu.VMEM((padded, cycle), f32),
            pltpu.VMEM((total_levels * SUB * COARSEN, LANES), f32),
            pltpu.VMEM((halves, wide_count * levels * line, LANES), f32),
            pltpu.VMEM((wide_count, halves, levels * line, LANES), f32),
            pltpu.VMEM((levels * ITEMS, padded, cycle), f32),
            pltpu.VMEM((groups * 4, rows, cycle), f32),
            pltpu.VMEM((wide_count, groups, rows, LANES), f32),
            pltpu.VMEM((wide_count, groups, rows, LANES), f32),
            pltpu.VMEM((wide_count, largest * fine_rows, LANES), f32),
            pltpu.VMEM((levels * ITEMS, SUB, cycle // 2), f32),
            pltpu.VMEM((levels * ITEMS, SUB, cycle // 2), f32),
            pltpu.VMEM((levels * ITEMS, SUB, cycle // 2), f32),
            pltpu.VMEM((levels * ITEMS, SUB, cycle // 2), f32),
            dma((halves, 2, 4)),
            dma((2 + halves,)),
            dma((2 * turns, wide_count)),
            dma((2 * turns, wide_count)),
            dma((turns, 2)),
            dma((turns, 2)),
            dma((turns, wide_count)),
            dma((turns, wide_count)),
        ],
        compiler_params=pltpu.CompilerParams(
            collective_id=0, has_side_effects=True, vmem_limit_bytes=40 * 1024 * 1024
        ),
        name="analysis",
    )(
        *(
            pltpu.with_memory_space_constraint(x, pltpu.HBM)
            for x in (
                trajectory,
                innovation.transpose(0, 2, 3, 1),
                background.transpose(0, 2, 3, 1),
                obs_weight.transpose(1, 2, 0),
                wave,
            )
        )
    )


def solution(mesh):
    in_specs = (
        P(None, None, "narrow", "wide"),
        P(None, None, "narrow", "wide"),
        P(None, None, "narrow", "wide"),
        P(None, "narrow", "wide"),
    )
    out_specs = P(None, None, "narrow", "wide")
    return jax.shard_map(shards, mesh=mesh, in_specs=in_specs, out_specs=out_specs, check_vma=False)
```
